512 devices in a mesh: fibre: 16 (over y, core), col: 32 (over x, z).
Axes of the slice: x: 4, y: 8, z: 8, core: 2. Of those that a mesh axis runs over, the one named last changes fastest.
Arguments:
- field: float32 [640, 160, 4096], P('fibre', None, 'col'), may hold values from -180 to 180, as said below
- start: float32 [640, 160], replicated, may hold values from -6 to 6
Outputs:
- basis: float32 [640, 160], replicated
- core: float32 [160, 160, 4096], P(None, 'fibre', 'col')
The draws below stay inside these ranges and needn't reach their ends.
Inputs may be any that keep to these rules, and one draw needn't show every extreme that they name: `field`: entries are finite real values.
All inputs are finite; a program needn't handle non-finite values.
Results may differ from the reference program's by a relative error of at most 0.00016.
Values sent between devices are 32-bit elements; how exact they have to be, the bound alone decides.
No kernel may reach another device: no remote copies, remote signals or barrier semaphores. Data moves between devices by JAX's collectives and lax.ppermute only.
A program may use at most 64 MiB of HBM per device.

```python
import jax
import jax.numpy as jnp
from jax import lax

I1 = 640
RANK = 160
ITERS = 2
P_SIZE = 160
Q = 4096


def draw_field(key, part):
    key_a = jax.random.fold_in(key, 11)
    key_b = jax.random.fold_in(key, 12)
    key_c = jax.random.fold_in(key, 13)
    entries = jnp.clip(jax.random.normal(key_a, (I1, P_SIZE, Q), jnp.float32), -6.0, 6.0)
    row_scale = jnp.exp(jax.random.uniform(key_b, (I1, 1, 1), jnp.float32, 0.0, jnp.log(3.0)))
    col_scale = jnp.exp(jax.random.uniform(key_c, (1, P_SIZE, Q), jnp.float32, jnp.log(0.3), jnp.log(3.0)))
    return entries * row_scale * col_scale


def gaussian(own_key, extent, deviation, bound, dtype=jnp.bfloat16):
    values = deviation * jax.random.normal(own_key, extent, jnp.float32)
    return jnp.clip(values, min=-bound, max=bound).astype(dtype)


def setup_inputs(seed: int = 0) -> dict:
    key_list = jax.random.split(jax.random.key(seed), 3)
    field = draw_field(jax.random.fold_in(key_list[2], 71), 0)
    start = gaussian(key_list[1], (I1, RANK), 1.0, 6.0, jnp.float32)
    return {"field": field, "start": start}


def subspace(gram, start):
    block = start
    for turn in range(ITERS):
        image = jnp.dot(gram.astype(jnp.float32), block.astype(jnp.float32), precision=lax.Precision.HIGHEST, preferred_element_type=jnp.float32)
        small = jnp.dot(image.T.astype(jnp.float32), image.astype(jnp.float32), precision=lax.Precision.HIGHEST, preferred_element_type=jnp.float32)
        factor = jnp.linalg.cholesky(small)
        block = lax.linalg.triangular_solve(factor, image, left_side=False, lower=True, transpose_a=True)
    return block

def reference(field, start):
    unfolded = field.reshape(field.shape[0], -1)
    gram = jnp.dot(unfolded.astype(jnp.float32), unfolded.T.astype(jnp.float32), precision=lax.Precision.HIGHEST, preferred_element_type=jnp.float32)
    basis = subspace(gram, start)
    core = jnp.dot(basis.T.astype(jnp.float32), unfolded.astype(jnp.float32), precision=lax.Precision.HIGHEST, preferred_element_type=jnp.float32)
    return (basis, core.reshape(basis.shape[1], field.shape[1], field.shape[2]))
```

```python
import functools
import jax, jax.numpy as jnp
from jax import lax
from jax.experimental import pallas as pl
from jax.experimental.pallas import tpu as pltpu
from jax.sharding import PartitionSpec as P
HI=lax.Precision.HIGHEST
f32=jnp.float32
NT=(((1,),(1,)),((),())); NN=(((1,),(0,)),((),())); TN=(((0,),(0,)),((),()))
def dot(a,b,d=NN,prec=HI): return lax.dot_general(a,b,d,precision=prec,preferred_element_type=f32)
NB=32
def inv_diag1(X,nb=NB):
    row=lax.broadcasted_iota(jnp.int32,(nb,1),0)
    for j in range(nb-1):
        t=(j+1)//8*8
        r=X[j:j+1,:]; c=X[t:,j:j+1]; p=X[j:j+1,j:j+1]
        m=jnp.where(row[t:]>j,c*(1.0/p),0.0)
        Y=X[t:]-m*r
        X=jnp.concatenate([X[:t],Y]) if t else Y
    lane=lax.broadcasted_iota(jnp.int32,(nb,128),1)
    rw=lax.broadcasted_iota(jnp.int32,(nb,128),0)
    d=jnp.sum(jnp.where(lane==rw,X,0.0),axis=1,keepdims=True)
    return X[:,nb:2*nb]*lax.rsqrt(d)
def orth(a_ref,t_ref,R,inv=inv_diag1):
    n=R//NB
    lane=lax.broadcasted_iota(jnp.int32,(NB,128),1)
    rw=lax.broadcasted_iota(jnp.int32,(NB,128),0)
    for k in range(n):
        rows=slice(k*NB,(k+1)*NB)
        base=k*NB//128*128; off=k*NB-base
        D=a_ref[rows,base:base+128]
        if off: D=pltpu.roll(D,128-off,1)
        X=jnp.where(lane<NB,D,jnp.where(lane-NB==rw,1.0,0.0))
        W=inv(X)
        if k<n-1:
            RA=dot(W,a_ref[rows,:])
            Q=dot(RA[:,:R],RA,TN)
            s=(k+1)*NB
            a_ref[s:,:]=a_ref[s:,:]-Q[s:,:]
        RT=dot(W,t_ref[rows,:])
        t_ref[rows,:]=RT
        if k<n-1:
            Q=dot(RA[:,:R],RT,TN)
            t_ref[s:,:]=t_ref[s:,:]-Q[s:,:]
def subspace(g_ref,a_ref,t_ref,R,iters,inv=inv_diag1):
    for it in range(iters):
        T=dot(t_ref[...],g_ref[...])
        t_ref[...]=T
        a_ref[:,:R]=dot(T,T,NT)
        orth(a_ref,t_ref,R,inv)
PAIRS=[(i,j) for i in range(5) for j in range(i,5)]
def unpack(p_ref,g_ref):
    for q,(i,j) in enumerate(PAIRS):
        b=p_ref[q]
        g_ref[i*128:(i+1)*128,j*128:(j+1)*128]=b
        if i!=j: g_ref[j*128:(j+1)*128,i*128:(i+1)*128]=b.T
def final_kernel(p_ref,s_ref,u_ref,basis_ref,core_ref,g_ref,a_ref,t_ref,*,inv=inv_diag1,corehi=HI):
    R=s_ref.shape[0]
    t_ref[...]=s_ref[...]
    unpack(p_ref,g_ref)
    a_ref[...]=jnp.zeros_like(a_ref)
    subspace(g_ref,a_ref,t_ref,R,2,inv)
    T=t_ref[...]
    basis_ref[...]=T
    for q in range(u_ref.shape[1]//2):
        U=jnp.concatenate([u_ref[:,2*q].reshape(640,128),u_ref[:,2*q+1].reshape(640,128)],axis=1)
        C=dot(T,U,NN,corehi)
        core_ref[2*q]=C[:,:128]; core_ref[2*q+1]=C[:,128:]
def final(p,s,u,**kw):
    return pl.pallas_call(functools.partial(final_kernel,**kw),
        out_shape=(jax.ShapeDtypeStruct((160,640),f32),jax.ShapeDtypeStruct((u.shape[1],160,128),f32)),
        in_specs=[pl.BlockSpec(memory_space=pltpu.VMEM)]*3,
        out_specs=(pl.BlockSpec(memory_space=pltpu.VMEM),)*2,
        scratch_shapes=[pltpu.VMEM((640,640),f32),pltpu.VMEM((160,256),f32),pltpu.VMEM((160,640),f32)],
        compiler_params=pltpu.CompilerParams(vmem_limit_bytes=48<<20))(p,s,u)
def split(x,n):
    out=[]
    for i in range(n):
        h=x.astype(jnp.bfloat16); out.append(h)
        if i<n-1: x=x-h.astype(f32)
    return out
def gram_kernel(u_ref,o_ref,*sc,n):
    np_=u_ref.shape[1]
    for p in range(np_):
        x=u_ref[:,p].reshape(640,128)
        for r,h in zip(sc,split(x,n)): r[:,p*128:(p+1)*128]=h
    prods=[(0,0),(0,1),(1,0)] if n==2 else [(0,0),(0,1),(1,0),(1,1),(0,2),(2,0)]
    q=0
    for i in range(5):
        acc=None
        for a,b in reversed(prods):
            t=lax.dot_general(sc[a][i*128:(i+1)*128,:],sc[b][i*128:,:],NT,preferred_element_type=f32)
            acc=t if acc is None else acc+t
        for j in range(i,5):
            o_ref[q]=acc[:,(j-i)*128:(j-i+1)*128]; q+=1
def gram(u,n=3):
    return pl.pallas_call(functools.partial(gram_kernel,n=n),
        out_shape=jax.ShapeDtypeStruct((15,128,128),f32),
        in_specs=[pl.BlockSpec(memory_space=pltpu.VMEM)],
        out_specs=pl.BlockSpec(memory_space=pltpu.VMEM),
        scratch_shapes=[pltpu.VMEM((640,u.shape[1]*128),jnp.bfloat16)]*n,
        compiler_params=pltpu.CompilerParams(vmem_limit_bytes=48<<20))(u)


FIBRE = ("y", "c")
NEAR = ("c", "x")
FAR = ("y", "z")


def exchange(pieces, axes):
    return lax.all_to_all(pieces, axes, 0, 0, tiled=True)


def sum_everywhere(packed):
    with jax.named_scope("reduce_near"):
        pieces = packed.reshape(8, 240, 128)
        mine = exchange(pieces, NEAR).sum(0)
    with jax.named_scope("reduce_far"):
        mine = jnp.pad(mine, ((0, 16), (0, 0))).reshape(64, 4, 128)
        mine = exchange(mine, FAR).sum(0)
    with jax.named_scope("gather_far"):
        mine = exchange(jnp.broadcast_to(mine, (64, 4, 128)), FAR)
        mine = mine.reshape(256, 128)[:240]
    with jax.named_scope("gather_near"):
        mine = lax.all_gather(mine, "x", axis=0, tiled=True)
        mine = lax.all_gather(mine, "c", axis=0, tiled=True)
    return mine.reshape(15, 128, 128)


def shards(field, start):
    with jax.named_scope("regroup"):
        pieces = field.transpose(1, 0, 2).reshape(16, 10, 40, 128)
        held = exchange(pieces, FIBRE)
    with jax.named_scope("gram"):
        local = gram(held)
    packed = sum_everywhere(local)
    with jax.named_scope("subspace"):
        basis, core = final(packed, start.T, held)
    return basis.T, core.transpose(1, 0, 2)


def solution(mesh):
    inner = jax.sharding.Mesh(mesh.devices.reshape(8, 2, 4, 8), ("y", "c", "x", "z"))
    return jax.shard_map(
        shards,
        mesh=inner,
        in_specs=(P(FIBRE, None, ("x", "z")), P()),
        out_specs=(P(), P(None, FIBRE, ("x", "z"))),
        check_vma=False,
    )
```

```python
import functools

import jax
import jax.numpy as jnp
from jax import lax
from jax.experimental import pallas as pl
from jax.experimental.pallas import tpu as pltpu
from jax.sharding import PartitionSpec as P

ITERS = 2
FIBRE = ("y", "c")
FAR = ("x", "y", "z")
SWAP = [(0, 1), (1, 0)]
NB = 40
STEP = 8
PAIRS = [(i, j) for i in range(5) for j in range(i, 5)]
VMEM = pl.BlockSpec(memory_space=pltpu.VMEM)
SMEM = pl.BlockSpec(memory_space=pltpu.SMEM)
ANY = pl.BlockSpec(memory_space=pl.ANY)
WHOLE = pltpu.CompilerParams(vmem_limit_bytes=60 << 20)
BIG = pltpu.CompilerParams(vmem_limit_bytes=24 << 20)
BF = jnp.bfloat16
F32 = jnp.float32
NN = (((1,), (0,)), ((), ()))
NT = (((1,), (1,)), ((), ()))
TN = (((0,), (0,)), ((), ()))


def dot(a, b, dims=NN):
    return lax.dot_general(
        a, b, dims, precision=lax.Precision.HIGHEST, preferred_element_type=F32
    )


def dot16(a, b, dims=NN):
    return lax.dot_general(a, b, dims, preferred_element_type=F32)


def halves(x):
    high = x.astype(BF)
    return high, (x - high.astype(F32)).astype(BF)


def regroup_kernel(field_ref, out_ref, sem):
    for p in range(field_ref.shape[1]):
        pltpu.make_async_copy(field_ref.at[:, p], out_ref.at[p], sem).start()
    pltpu.make_async_copy(out_ref, out_ref, sem).wait()


def regroup(field):
    rows, cells, lanes = field.shape
    return pl.pallas_call(
        regroup_kernel,
        out_shape=jax.ShapeDtypeStruct((cells, rows, lanes), F32),
        in_specs=[ANY],
        out_specs=ANY,
        scratch_shapes=[pltpu.SemaphoreType.DMA],
        compiler_params=WHOLE,
    )(field)


def gram_kernel(core_ref, held_ref, out_ref, high_ref, low_ref):
    for p in range(held_ref.shape[1]):
        x = held_ref[:, p].reshape(640, 128)
        high_ref[:, p * 128 : (p + 1) * 128], low_ref[:, p * 128 : (p + 1) * 128] = halves(x)
    core = core_ref[0]
    for slot in range(2):
        out_ref[slot, 960:, :] = jnp.zeros((64, 128), F32)
    block = 0
    for i in range(5):
        rows = slice(i * 128, (i + 1) * 128)
        both = jnp.concatenate([high_ref[rows, :], low_ref[rows, :]])
        by_high = dot16(both, high_ref[i * 128 :, :], NT)
        by_low = dot16(both, low_ref[i * 128 :, :], NT)
        product = (by_high[128:] + by_low[:128] + by_low[128:]) + by_high[:128]
        for j in range(5 - i):
            for part in range(2):
                piece = 2 * block + part
                at = piece % 15 * 64
                slot = core if piece < 15 else 1 - core
                out_ref[slot, at : at + 64, :] = product[
                    part * 64 : (part + 1) * 64, j * 128 : (j + 1) * 128
                ]
            block += 1


def local_gram(core, held):
    flat = jax.ShapeDtypeStruct((640, held.shape[1] * 128), BF)
    return pl.pallas_call(
        gram_kernel,
        out_shape=(jax.ShapeDtypeStruct((2, 1024, 128), F32), flat, flat),
        in_specs=[SMEM, VMEM],
        out_specs=(VMEM,) * 3,
        compiler_params=BIG,
    )(core, held)


def eliminate(square, w_ref):
    count = NB // 8
    tiles = [square[8 * t : 8 * t + 8] for t in range(count)]
    for j in range(0, NB, STEP):
        t0 = j // 8
        cols = [
            [jnp.broadcast_to(tiles[t][:, j + k : j + k + 1], (8, 128)) for t in range(t0, count)]
            for k in range(STEP)
        ]
        rows = [tiles[(j + k) // 8][(j + k) % 8 : (j + k) % 8 + 1, :] for k in range(STEP)]
        a = {
            (i, k): cols[k][(j + i) // 8 - t0][(j + i) % 8 : (j + i) % 8 + 1, :]
            for k in range(STEP)
            for i in range(k, STEP)
        }
        for k in range(STEP):
            scale = lax.rsqrt(a[k, k])
            rows[k] = rows[k] * scale
            for i in range(k + 1, STEP):
                a[i, k] = a[i, k] * scale
            for i in range(k + 1, STEP):
                for m in range(k + 1, i + 1):
                    a[i, m] = a[i, m] - a[i, k] * a[m, k]
            for i in range(k + 1, STEP):
                rows[i] = rows[i] - a[i, k] * rows[k]
            cols[k] = [c * scale for c in cols[k]]
            for i in range(k + 1, STEP):
                cols[i] = [c - a[i, k] * w for c, w in zip(cols[i], cols[k])]
            w_ref[j + k : j + k + 1, :] = rows[k]
        for t in range((j + STEP) // 8, count):
            change = cols[0][t - t0] * rows[0]
            for k in range(1, STEP):
                change = change + cols[k][t - t0] * rows[k]
            tiles[t] = tiles[t] - change
    return w_ref[:, NB : 2 * NB]


def orthonormalize(a_ref, t_ref, w_ref):
    rank = t_ref.shape[0]
    lane = lax.broadcasted_iota(jnp.int32, (NB, 128), 1)
    row = lax.broadcasted_iota(jnp.int32, (NB, 128), 0)
    for k in range(rank // NB):
        own = slice(k * NB, (k + 1) * NB)
        rest = (k + 1) * NB
        base = k * NB // 128 * 128
        off = k * NB - base
        block = a_ref[own, base : base + 128]
        if off:
            block = pltpu.roll(block, 128 - off, 1)
        if off + NB > 128:
            after = pltpu.roll(a_ref[own, base + 128 : base + 256], 128 - off, 1)
            block = jnp.where(lane < 128 - off, block, after)
        square = jnp.where(lane < NB, block, jnp.where(lane - NB == row, 1.0, 0.0))
        w = eliminate(square, w_ref.at[k % 2])
        if rest < rank:
            upper = dot(w, a_ref[own, :])
            change = dot(upper[:, :rank], upper, TN)
            a_ref[rest:, :] = a_ref[rest:, :] - change[rest:, :]
        solved = dot(w, t_ref[own, :])
        t_ref[own, :] = solved
        if rest < rank:
            change = dot(upper[:, :rank], solved, TN)
            t_ref[rest:, :] = t_ref[rest:, :] - change[rest:, :]


def subspace_kernel(
    packed_ref, start_ref, high_ref, low_ref, basis_ref, core_ref, g_ref, a_ref, t_ref, w_ref
):
    rank = start_ref.shape[0]
    for q, (i, j) in enumerate(PAIRS):
        block = packed_ref[q]
        g_ref[i * 128 : (i + 1) * 128, j * 128 : (j + 1) * 128] = block
        if i != j:
            g_ref[j * 128 : (j + 1) * 128, i * 128 : (i + 1) * 128] = block.T
    t_ref[...] = start_ref[...]
    a_ref[...] = jnp.zeros_like(a_ref)
    for _ in range(ITERS):
        image = dot(t_ref[...], g_ref[...])
        t_ref[...] = image
        a_ref[:, :rank] = dot(image, image, NT)
        orthonormalize(a_ref, t_ref, w_ref)
    basis = t_ref[...]
    basis_ref[...] = basis
    high, low = halves(basis)
    both = jnp.concatenate([high, low])
    for q in range(high_ref.shape[1] // 256):
        lanes = slice(q * 256, (q + 1) * 256)
        by_high = dot16(both, high_ref[:, lanes])
        by_low = dot16(high, low_ref[:, lanes])
        product = (by_high[rank:] + by_low) + by_high[:rank]
        core_ref[2 * q] = product[:, :128]
        core_ref[2 * q + 1] = product[:, 128:]


def subspace_and_core(packed, start, high, low):
    rank, rows = start.shape
    cells = high.shape[1] // 128
    return pl.pallas_call(
        subspace_kernel,
        out_shape=(
            jax.ShapeDtypeStruct((rank, rows), F32),
            jax.ShapeDtypeStruct((cells, rank, 128), F32),
        ),
        in_specs=[VMEM] * 4,
        out_specs=(VMEM,) * 2,
        scratch_shapes=[
            pltpu.VMEM((rows, rows), F32),
            pltpu.VMEM((rank, 256), F32),
            pltpu.VMEM((rank, rows), F32),
            pltpu.VMEM((2, NB, 128), F32),
        ],
        compiler_params=BIG,
    )(packed, start, high, low)


def exchange(pieces, axes):
    return lax.all_to_all(pieces, axes, 0, 0, tiled=True)


def shards(field, start):
    with jax.named_scope("regroup"):
        pieces = regroup(field).reshape(16, 10, 40, 128)
        held = exchange(pieces, FIBRE)
    with jax.named_scope("gram"):
        core = lax.axis_index("c").astype(jnp.int32).reshape(1)
        parts, high, low = local_gram(core, held)
    with jax.named_scope("reduce_pair"):
        mine = parts[0] + lax.ppermute(parts[1], "c", SWAP)
    with jax.named_scope("reduce_far"):
        mine = exchange(mine.reshape(256, 4, 128), FAR).sum(0)
    with jax.named_scope("gather_far"):
        mine = exchange(jnp.broadcast_to(mine, (256, 4, 128)), FAR)
        mine = mine[:240].reshape(960, 128)
    with jax.named_scope("gather_pair"):
        packed = lax.all_gather(mine, "c", axis=0, tiled=True).reshape(15, 128, 128)
    with jax.named_scope("subspace"):
        basis, core = subspace_and_core(packed, start.T, high, low)
    return basis.T, core.transpose(1, 0, 2)


def solution(mesh):
    inner = jax.sharding.Mesh(mesh.devices.reshape(8, 2, 4, 8), ("y", "c", "x", "z"))
    return jax.shard_map(
        shards,
        mesh=inner,
        in_specs=(P(FIBRE, None, ("x", "z")), P()),
        out_specs=(P(), P(None, FIBRE, ("x", "z"))),
        check_vma=False,
    )
```

```python
import functools

import jax
import jax.numpy as jnp
from jax import lax
from jax.experimental import pallas as pl
from jax.experimental.pallas import tpu as pltpu
from jax.sharding import PartitionSpec as P

ITERS = 2
FIBRE = ("y", "c")
PLANE = ("z", "x")
SWAP = [(0, 1), (1, 0)]
NB = 40
STEP = 8
PAIRS = [(i, j) for i in range(5) for j in range(i, 5)]
VMEM = pl.BlockSpec(memory_space=pltpu.VMEM)
HBM = pl.BlockSpec(memory_space=pltpu.HBM)
SMEM = pl.BlockSpec(memory_space=pltpu.SMEM)
WHOLE = pltpu.CompilerParams(vmem_limit_bytes=56 << 20)
BIG = pltpu.CompilerParams(vmem_limit_bytes=24 << 20)
BF = jnp.bfloat16
F32 = jnp.float32
NN = (((1,), (0,)), ((), ()))
NT = (((1,), (1,)), ((), ()))
TN = (((0,), (0,)), ((), ()))


def dot(a, b, dims=NN):
    return lax.dot_general(
        a, b, dims, precision=lax.Precision.HIGHEST, preferred_element_type=F32
    )


def dot16(a, b, dims=NN):
    return lax.dot_general(a, b, dims, preferred_element_type=F32)


def halves(x):
    high = x.astype(BF)
    return high, (x - high.astype(F32)).astype(BF)


def regroup_kernel(field_ref, out_ref):
    out_ref[...] = jnp.swapaxes(field_ref[...], 0, 1)


def regroup(field):
    rows, cells, lanes = field.shape
    return pl.pallas_call(
        regroup_kernel,
        grid=(rows // 8,),
        out_shape=jax.ShapeDtypeStruct((cells, rows, lanes), F32),
        in_specs=[pl.BlockSpec((8, cells, lanes), lambda i: (i, 0, 0))],
        out_specs=pl.BlockSpec((cells, 8, lanes), lambda i: (0, i, 0)),
        compiler_params=WHOLE,
    )(field)


def gram_kernel(core_ref, held_ref, out_ref, high_out, low_out, high_ref, low_ref, sem):
    for p in range(held_ref.shape[1]):
        x = held_ref[:, p].reshape(640, 128)
        high_ref[:, p * 128 : (p + 1) * 128], low_ref[:, p * 128 : (p + 1) * 128] = halves(x)
    copies = [
        pltpu.make_async_copy(high_ref, high_out, sem.at[0]),
        pltpu.make_async_copy(low_ref, low_out, sem.at[1]),
    ]
    for copy in copies:
        copy.start()
    core = core_ref[0]
    for slot in range(2):
        out_ref[slot, 960:, :] = jnp.zeros((64, 128), F32)
    block = 0
    for i in range(5):
        rows = slice(i * 128, (i + 1) * 128)
        both = jnp.concatenate([high_ref[rows, :], low_ref[rows, :]])
        by_high = dot16(both, high_ref[i * 128 :, :], NT)
        by_low = dot16(both, low_ref[i * 128 :, :], NT)
        product = (by_high[128:] + by_low[:128] + by_low[128:]) + by_high[:128]
        for j in range(5 - i):
            for part in range(2):
                piece = 2 * block + part
                at = piece % 15 * 64
                slot = core if piece < 15 else 1 - core
                out_ref[slot, at : at + 64, :] = product[
                    part * 64 : (part + 1) * 64, j * 128 : (j + 1) * 128
                ]
            block += 1
    for copy in copies:
        copy.wait()


def local_gram(core, held):
    flat = jax.ShapeDtypeStruct((640, held.shape[1] * 128), BF)
    return pl.pallas_call(
        gram_kernel,
        out_shape=(jax.ShapeDtypeStruct((2, 1024, 128), F32), pltpu.HBM(flat.shape, BF), pltpu.HBM(flat.shape, BF)),
        in_specs=[SMEM, VMEM],
        out_specs=(VMEM, HBM, HBM),
        scratch_shapes=[
            pltpu.VMEM(flat.shape, BF),
            pltpu.VMEM(flat.shape, BF),
            pltpu.SemaphoreType.DMA((2,)),
        ],
        compiler_params=BIG,
    )(core, held)


def eliminate(square, w_ref):
    count = NB // 8
    tiles = [square[8 * t : 8 * t + 8] for t in range(count)]
    for j in range(0, NB, STEP):
        t0 = j // 8
        cols = [
            [jnp.broadcast_to(tiles[t][:, j + k : j + k + 1], (8, 128)) for t in range(t0, count)]
            for k in range(STEP)
        ]
        rows = [tiles[(j + k) // 8][(j + k) % 8 : (j + k) % 8 + 1, :] for k in range(STEP)]
        a = {
            (i, k): cols[k][(j + i) // 8 - t0][(j + i) % 8 : (j + i) % 8 + 1, :]
            for k in range(STEP)
            for i in range(k, STEP)
        }
        for k in range(STEP):
            scale = lax.rsqrt(a[k, k])
            rows[k] = rows[k] * scale
            for i in range(k + 1, STEP):
                a[i, k] = a[i, k] * scale
            for i in range(k + 1, STEP):
                for m in range(k + 1, i + 1):
                    a[i, m] = a[i, m] - a[i, k] * a[m, k]
            for i in range(k + 1, STEP):
                rows[i] = rows[i] - a[i, k] * rows[k]
            cols[k] = [c * scale for c in cols[k]]
            for i in range(k + 1, STEP):
                cols[i] = [c - a[i, k] * w for c, w in zip(cols[i], cols[k])]
            w_ref[j + k : j + k + 1, :] = rows[k]
        for t in range((j + STEP) // 8, count):
            change = cols[0][t - t0] * rows[0]
            for k in range(1, STEP):
                change = change + cols[k][t - t0] * rows[k]
            tiles[t] = tiles[t] - change
    return w_ref[:, NB : 2 * NB]


def orthonormalize(a_ref, t_ref, w_ref):
    rank = t_ref.shape[0]
    lane = lax.broadcasted_iota(jnp.int32, (NB, 128), 1)
    row = lax.broadcasted_iota(jnp.int32, (NB, 128), 0)
    for k in range(rank // NB):
        own = slice(k * NB, (k + 1) * NB)
        rest = (k + 1) * NB
        base = k * NB // 128 * 128
        off = k * NB - base
        block = a_ref[own, base : base + 128]
        if off:
            block = pltpu.roll(block, 128 - off, 1)
        if off + NB > 128:
            after = pltpu.roll(a_ref[own, base + 128 : base + 256], 128 - off, 1)
            block = jnp.where(lane < 128 - off, block, after)
        square = jnp.where(lane < NB, block, jnp.where(lane - NB == row, 1.0, 0.0))
        w = eliminate(square, w_ref.at[k % 2])
        if rest < rank:
            upper = dot(w, a_ref[own, :])
            change = dot(upper[:, :rank], upper, TN)
            a_ref[rest:, :] = a_ref[rest:, :] - change[rest:, :]
        solved = dot(w, t_ref[own, :])
        t_ref[own, :] = solved
        if rest < rank:
            change = dot(upper[:, :rank], solved, TN)
            t_ref[rest:, :] = t_ref[rest:, :] - change[rest:, :]


def subspace_kernel(
    packed_ref,
    start_ref,
    high_in,
    low_in,
    basis_out,
    core_out,
    g_ref,
    a_ref,
    t_ref,
    w_ref,
    high_ref,
    low_ref,
    core_ref,
    sem,
):
    rank = start_ref.shape[0]
    pairs = high_ref.shape[1] // 256
    loads = [
        pltpu.make_async_copy(high_in, high_ref, sem.at[0]),
        pltpu.make_async_copy(low_in, low_ref, sem.at[1]),
    ]
    for copy in loads:
        copy.start()
    for q, (i, j) in enumerate(PAIRS):
        block = packed_ref[q]
        g_ref[i * 128 : (i + 1) * 128, j * 128 : (j + 1) * 128] = block
        if i != j:
            g_ref[j * 128 : (j + 1) * 128, i * 128 : (i + 1) * 128] = block.T
    t_ref[...] = start_ref[...]
    a_ref[...] = jnp.zeros_like(a_ref)
    for _ in range(ITERS):
        image = dot(t_ref[...], g_ref[...])
        t_ref[...] = image
        a_ref[:, :rank] = dot(image, image, NT)
        orthonormalize(a_ref, t_ref, w_ref)
    basis = t_ref[...]
    stores = [pltpu.make_async_copy(t_ref, basis_out, sem.at[2])]
    stores[0].start()
    for copy in loads:
        copy.wait()
    high, low = halves(basis)
    both = jnp.concatenate([high, low])
    for q in range(pairs):
        lanes = slice(q * 256, (q + 1) * 256)
        by_high = dot16(both, high_ref[:, lanes])
        by_low = dot16(high, low_ref[:, lanes])
        product = (by_high[rank:] + by_low) + by_high[:rank]
        core_ref[2 * q] = product[:, :128]
        core_ref[2 * q + 1] = product[:, 128:]
        two = pl.ds(2 * q, 2)
        stores.append(pltpu.make_async_copy(core_ref.at[two], core_out.at[two], sem.at[3 + q]))
        stores[-1].start()
    for copy in stores:
        copy.wait()


def subspace_and_core(packed, start, high, low):
    rank, rows = start.shape
    cells = high.shape[1] // 128
    return pl.pallas_call(
        subspace_kernel,
        out_shape=(
            jax.ShapeDtypeStruct((rank, rows), F32),
            jax.ShapeDtypeStruct((cells, rank, 128), F32),
        ),
        in_specs=[VMEM, VMEM, HBM, HBM],
        out_specs=(HBM, HBM),
        scratch_shapes=[
            pltpu.VMEM((rows, rows), F32),
            pltpu.VMEM((rank, 256), F32),
            pltpu.VMEM((rank, rows), F32),
            pltpu.VMEM((2, NB, 128), F32),
            pltpu.VMEM(high.shape, BF),
            pltpu.VMEM(low.shape, BF),
            pltpu.VMEM((cells, rank, 128), F32),
            pltpu.SemaphoreType.DMA((3 + cells // 2,)),
        ],
        compiler_params=BIG,
    )(packed, start, *(pltpu.with_memory_space_constraint(v, pltpu.HBM) for v in (high, low)))


def exchange(pieces, axes):
    return lax.all_to_all(pieces, axes, 0, 0, tiled=True)


def shards(field, start):
    with jax.named_scope("regroup"):
        pieces = regroup(field).reshape(16, 10, 40, 128)
        held = exchange(pieces, FIBRE)
    with jax.named_scope("gram"):
        core = lax.axis_index("c").astype(jnp.int32).reshape(1)
        parts, high, low = local_gram(core, held)
    with jax.named_scope("reduce_pair"):
        mine = parts[0] + lax.ppermute(parts[1], "c", SWAP)
    with jax.named_scope("reduce_plane"):
        mine = exchange(mine.reshape(32, 32, 128), PLANE).sum(0)
    with jax.named_scope("sum_line"):
        mine = exchange(jnp.broadcast_to(mine, (8, 32, 128)), "y").sum(0)
    with jax.named_scope("gather_plane"):
        mine = exchange(jnp.broadcast_to(mine, (32, 32, 128)), PLANE)
        mine = mine.reshape(1024, 128)[:960]
    with jax.named_scope("gather_pair"):
        packed = lax.all_gather(mine, "c", axis=0, tiled=True).reshape(15, 128, 128)
    with jax.named_scope("subspace"):
        basis, core = subspace_and_core(packed, start.T, high, low)
    return basis.T, core.transpose(1, 0, 2)


def solution(mesh):
    inner = jax.sharding.Mesh(mesh.devices.reshape(8, 2, 4, 8), ("y", "c", "x", "z"))
    return jax.shard_map(
        shards,
        mesh=inner,
        in_specs=(P(FIBRE, None, ("x", "z")), P()),
        out_specs=(P(), P(None, FIBRE, ("x", "z"))),
        check_vma=False,
    )
```

```python
import functools

import jax
import jax.numpy as jnp
from jax import lax
from jax.experimental import pallas as pl
from jax.experimental.pallas import tpu as pltpu
from jax.sharding import PartitionSpec as P

ITERS = 2
FIBRE = ("y", "c")
PLANE = ("z", "x")
SWAP = [(0, 1), (1, 0)]
NB = 40
STEP = 8
UPPER = [20, 21, 22, 23, 24]
ACROSS = {
    pair: 2 * at
    for at, pair in enumerate((i, j) for i in range(5) for j in range(i + 1, 5))
}
VMEM = pl.BlockSpec(memory_space=pltpu.VMEM)
HBM = pl.BlockSpec(memory_space=pltpu.HBM)
SMEM = pl.BlockSpec(memory_space=pltpu.SMEM)
BIG = pltpu.CompilerParams(vmem_limit_bytes=24 << 20)
BF = jnp.bfloat16
F32 = jnp.float32
NN = (((1,), (0,)), ((), ()))
NT = (((1,), (1,)), ((), ()))
TN = (((0,), (0,)), ((), ()))


def dot(a, b, dims=NN):
    return lax.dot_general(
        a, b, dims, precision=lax.Precision.HIGHEST, preferred_element_type=F32
    )


def dot16(a, b, dims=NN):
    return lax.dot_general(a, b, dims, preferred_element_type=F32)


def halves(x):
    high = x.astype(BF)
    return high, (x - high.astype(F32)).astype(BF)


def gram_kernel(core_ref, held_ref, out_ref, high_out, low_out, high_ref, low_ref, sem):
    for p in range(held_ref.shape[1]):
        x = held_ref[:, p].reshape(640, 128)
        high_ref[:, p * 128 : (p + 1) * 128], low_ref[:, p * 128 : (p + 1) * 128] = halves(x)
    copies = [
        pltpu.make_async_copy(high_ref, high_out, sem.at[0]),
        pltpu.make_async_copy(low_ref, low_out, sem.at[1]),
    ]
    for copy in copies:
        copy.start()
    core = core_ref[0]

    def put(strip, value):
        at = strip % 14 * 64
        out_ref[core if strip < 14 else 1 - core, at : at + 64, :] = value

    lower = []
    for i in range(5):
        rows = slice(i * 128, (i + 1) * 128)
        both = jnp.concatenate([high_ref[rows, :], low_ref[rows, :]])
        by_high = dot16(both, high_ref[i * 128 :, :], NT)
        by_low = dot16(both, low_ref[i * 128 :, :], NT)
        product = (by_high[128:] + by_low[:128] + by_low[128:]) + by_high[:128]
        for j in range(i, 5):
            block = product[:, (j - i) * 128 : (j - i + 1) * 128]
            if i == j:
                put(UPPER[i], block[:64])
                lower.append(block[64:])
            else:
                put(ACROSS[i, j], block[:64])
                put(ACROSS[i, j] + 1, block[64:])
    left = lax.broadcasted_iota(jnp.int32, (64, 128), 1) < 64
    put(25, jnp.where(left, pltpu.roll(lower[1], 64, 1), lower[0]))
    put(26, jnp.where(left, pltpu.roll(lower[3], 64, 1), lower[2]))
    put(27, lower[4])
    for copy in copies:
        copy.wait()


def local_gram(core, held):
    flat = jax.ShapeDtypeStruct((640, held.shape[1] * 128), BF)
    return pl.pallas_call(
        gram_kernel,
        out_shape=(jax.ShapeDtypeStruct((2, 896, 128), F32), pltpu.HBM(flat.shape, BF), pltpu.HBM(flat.shape, BF)),
        in_specs=[SMEM, VMEM],
        out_specs=(VMEM, HBM, HBM),
        scratch_shapes=[
            pltpu.VMEM(flat.shape, BF),
            pltpu.VMEM(flat.shape, BF),
            pltpu.SemaphoreType.DMA((2,)),
        ],
        compiler_params=BIG,
    )(core, held)


def eliminate(square, w_ref):
    count = NB // 8
    tiles = [square[8 * t : 8 * t + 8] for t in range(count)]
    for j in range(0, NB, STEP):
        t0 = j // 8
        cols = [
            [jnp.broadcast_to(tiles[t][:, j + k : j + k + 1], (8, 128)) for t in range(t0, count)]
            for k in range(STEP)
        ]
        rows = [tiles[(j + k) // 8][(j + k) % 8 : (j + k) % 8 + 1, :] for k in range(STEP)]
        a = {
            (i, k): cols[k][(j + i) // 8 - t0][(j + i) % 8 : (j + i) % 8 + 1, :]
            for k in range(STEP)
            for i in range(k, STEP)
        }
        for k in range(STEP):
            scale = lax.rsqrt(a[k, k])
            rows[k] = rows[k] * scale
            for i in range(k + 1, STEP):
                a[i, k] = a[i, k] * scale
            for i in range(k + 1, STEP):
                for m in range(k + 1, i + 1):
                    a[i, m] = a[i, m] - a[i, k] * a[m, k]
            for i in range(k + 1, STEP):
                rows[i] = rows[i] - a[i, k] * rows[k]
            cols[k] = [c * scale for c in cols[k]]
            for i in range(k + 1, STEP):
                cols[i] = [c - a[i, k] * w for c, w in zip(cols[i], cols[k])]
            w_ref[j + k : j + k + 1, :] = rows[k]
        for t in range((j + STEP) // 8, count):
            change = cols[0][t - t0] * rows[0]
            for k in range(1, STEP):
                change = change + cols[k][t - t0] * rows[k]
            tiles[t] = tiles[t] - change
    return w_ref[:, NB : 2 * NB]


def orthonormalize(a_ref, t_ref, w_ref):
    rank = t_ref.shape[0]
    lane = lax.broadcasted_iota(jnp.int32, (NB, 128), 1)
    row = lax.broadcasted_iota(jnp.int32, (NB, 128), 0)
    for k in range(rank // NB):
        own = slice(k * NB, (k + 1) * NB)
        rest = (k + 1) * NB
        base = k * NB // 128 * 128
        off = k * NB - base
        block = a_ref[own, base : base + 128]
        if off:
            block = pltpu.roll(block, 128 - off, 1)
        if off + NB > 128:
            after = pltpu.roll(a_ref[own, base + 128 : base + 256], 128 - off, 1)
            block = jnp.where(lane < 128 - off, block, after)
        square = jnp.where(lane < NB, block, jnp.where(lane - NB == row, 1.0, 0.0))
        w = eliminate(square, w_ref.at[k % 2])
        if rest < rank:
            upper = dot(w, a_ref[own, :])
            change = dot(upper[:, :rank], upper, TN)
            a_ref[rest:, :] = a_ref[rest:, :] - change[rest:, :]
        solved = dot(w, t_ref[own, :])
        t_ref[own, :] = solved
        if rest < rank:
            change = dot(upper[:, :rank], solved, TN)
            t_ref[rest:, :] = t_ref[rest:, :] - change[rest:, :]


def subspace_kernel(
    packed_ref,
    start_ref,
    high_in,
    low_in,
    basis_out,
    core_out,
    g_ref,
    a_ref,
    t_ref,
    w_ref,
    high_ref,
    low_ref,
    core_ref,
    sem,
):
    rank = start_ref.shape[0]
    pairs = high_ref.shape[1] // 256
    loads = [
        pltpu.make_async_copy(high_in, high_ref, sem.at[0]),
        pltpu.make_async_copy(low_in, low_ref, sem.at[1]),
    ]
    for copy in loads:
        copy.start()
    for (i, j), at in ACROSS.items():
        block = packed_ref[at * 64 : at * 64 + 128, :]
        g_ref[i * 128 : (i + 1) * 128, j * 128 : (j + 1) * 128] = block
        g_ref[j * 128 : (j + 1) * 128, i * 128 : (i + 1) * 128] = block.T
    right = lax.broadcasted_iota(jnp.int32, (64, 128), 1) >= 64
    for i in range(5):
        upper = packed_ref[UPPER[i] * 64 : UPPER[i] * 64 + 64, :]
        lower = packed_ref[(25 + i // 2) * 64 : (26 + i // 2) * 64, :]
        if i % 2:
            lower = pltpu.roll(lower, 64, 1)
        turned = jnp.concatenate([upper, upper]).T[64:]
        square = slice(i * 128, (i + 1) * 128)
        g_ref[square, square] = jnp.concatenate([upper, jnp.where(right, lower, turned)])
    t_ref[...] = start_ref[...]
    a_ref[...] = jnp.zeros_like(a_ref)
    for _ in range(ITERS):
        image = dot(t_ref[...], g_ref[...])
        t_ref[...] = image
        a_ref[:, :rank] = dot(image, image, NT)
        orthonormalize(a_ref, t_ref, w_ref)
    basis = t_ref[...]
    stores = [pltpu.make_async_copy(t_ref, basis_out, sem.at[2])]
    stores[0].start()
    for copy in loads:
        copy.wait()
    high, low = halves(basis)
    both = jnp.concatenate([high, low])
    for q in range(pairs):
        lanes = slice(q * 256, (q + 1) * 256)
        by_high = dot16(both, high_ref[:, lanes])
        by_low = dot16(high, low_ref[:, lanes])
        product = (by_high[rank:] + by_low) + by_high[:rank]
        core_ref[2 * q] = product[:, :128]
        core_ref[2 * q + 1] = product[:, 128:]
        two = pl.ds(2 * q, 2)
        stores.append(pltpu.make_async_copy(core_ref.at[two], core_out.at[two], sem.at[3 + q]))
        stores[-1].start()
    for copy in stores:
        copy.wait()


def subspace_and_core(packed, start, high, low):
    rank, rows = start.shape
    cells = high.shape[1] // 128
    return pl.pallas_call(
        subspace_kernel,
        out_shape=(
            jax.ShapeDtypeStruct((rank, rows), F32),
            jax.ShapeDtypeStruct((cells, rank, 128), F32),
        ),
        in_specs=[VMEM, VMEM, HBM, HBM],
        out_specs=(HBM, HBM),
        scratch_shapes=[
            pltpu.VMEM((rows, rows), F32),
            pltpu.VMEM((rank, 256), F32),
            pltpu.VMEM((rank, rows), F32),
            pltpu.VMEM((2, NB, 128), F32),
            pltpu.VMEM(high.shape, BF),
            pltpu.VMEM(low.shape, BF),
            pltpu.VMEM((cells, rank, 128), F32),
            pltpu.SemaphoreType.DMA((3 + cells // 2,)),
        ],
        compiler_params=BIG,
    )(packed, start, *(pltpu.with_memory_space_constraint(v, pltpu.HBM) for v in (high, low)))


def exchange(pieces, axes):
    return lax.all_to_all(pieces, axes, 0, 0, tiled=True)


def shards(field, start):
    with jax.named_scope("regroup"):
        pieces = field.transpose(1, 0, 2).reshape(16, 10, 40, 128)
        held = exchange(pieces, FIBRE)
    with jax.named_scope("gram"):
        core = lax.axis_index("c").astype(jnp.int32).reshape(1)
        parts, high, low = local_gram(core, held)
    with jax.named_scope("reduce_pair"):
        mine = parts[0] + lax.ppermute(parts[1], "c", SWAP)
    with jax.named_scope("reduce_plane"):
        mine = exchange(mine.reshape(32, 7, 4, 128), PLANE).sum(0)
    with jax.named_scope("sum_line"):
        mine = exchange(jnp.broadcast_to(mine, (8, 7, 4, 128)), "y").sum(0)
    with jax.named_scope("gather_plane"):
        mine = exchange(jnp.broadcast_to(mine, (32, 7, 4, 128)), PLANE)
    with jax.named_scope("gather_pair"):
        packed = lax.all_gather(mine.reshape(896, 128), "c", axis=0, tiled=True)
    with jax.named_scope("subspace"):
        basis, core = subspace_and_core(packed, start.T, high, low)
    return basis.T, core.transpose(1, 0, 2)


def solution(mesh):
    inner = jax.sharding.Mesh(mesh.devices.reshape(8, 2, 4, 8), ("y", "c", "x", "z"))
    return jax.shard_map(
        shards,
        mesh=inner,
        in_specs=(P(FIBRE, None, ("x", "z")), P()),
        out_specs=(P(), P(None, FIBRE, ("x", "z"))),
        check_vma=False,
    )
```

```python
import functools

import jax
import jax.numpy as jnp
from jax import lax
from jax.experimental import pallas as pl
from jax.experimental.pallas import tpu as pltpu
from jax.sharding import PartitionSpec as P

ITERS = 2
FIBRE = ("y", "c")
PLANE = ("z", "x")
SWAP = [(0, 1), (1, 0)]
NB = 40
STEP = 8
UPPER = [20, 21, 22, 23, 24]
ACROSS = {
    pair: 2 * at
    for at, pair in enumerate((i, j) for i in range(5) for j in range(i + 1, 5))
}
VMEM = pl.BlockSpec(memory_space=pltpu.VMEM)
HBM = pl.BlockSpec(memory_space=pltpu.HBM)
SMEM = pl.BlockSpec(memory_space=pltpu.SMEM)
BIG = pltpu.CompilerParams(vmem_limit_bytes=24 << 20)
BF = jnp.bfloat16
F32 = jnp.float32
NN = (((1,), (0,)), ((), ()))
NT = (((1,), (1,)), ((), ()))
TN = (((0,), (0,)), ((), ()))


def dot(a, b, dims=NN):
    return lax.dot_general(
        a, b, dims, precision=lax.Precision.HIGHEST, preferred_element_type=F32
    )


def dot16(a, b, dims=NN):
    return lax.dot_general(a, b, dims, preferred_element_type=F32)


def halves(x):
    high = x.astype(BF)
    return high, (x - high.astype(F32)).astype(BF)


def regroup_kernel(field_ref, out_ref, in_ref, sem):
    parts = field_ref.shape[0] // 8
    copies = []
    for part in range(parts):
        rows = pl.ds(8 * part, 8)
        copies.append(
            pltpu.make_async_copy(field_ref.at[rows], in_ref.at[rows], sem.at[part])
        )
        copies[-1].start()
    for part, copy in enumerate(copies):
        copy.wait()
        rows = slice(8 * part, 8 * part + 8)
        out_ref[:, rows, :] = jnp.swapaxes(in_ref[rows], 0, 1)


def regroup(field):
    rows, cells, lanes = field.shape
    return pl.pallas_call(
        regroup_kernel,
        out_shape=jax.ShapeDtypeStruct((cells, rows, lanes), F32),
        in_specs=[HBM],
        out_specs=VMEM,
        scratch_shapes=[pltpu.VMEM(field.shape, F32), pltpu.SemaphoreType.DMA((rows // 8,))],
        compiler_params=BIG,
    )(pltpu.with_memory_space_constraint(field, pltpu.HBM))


def gram_kernel(core_ref, held_ref, out_ref, high_out, low_out, high_ref, low_ref, sem):
    for p in range(held_ref.shape[1]):
        x = held_ref[:, p].reshape(640, 128)
        high_ref[:, p * 128 : (p + 1) * 128], low_ref[:, p * 128 : (p + 1) * 128] = halves(x)
    copies = [
        pltpu.make_async_copy(high_ref, high_out, sem.at[0]),
        pltpu.make_async_copy(low_ref, low_out, sem.at[1]),
    ]
    for copy in copies:
        copy.start()
    core = core_ref[0]

    def put(strip, value):
        at = strip % 14 * 64
        out_ref[core if strip < 14 else 1 - core, at : at + 64, :] = value

    lower = []
    for i in range(5):
        rows = slice(i * 128, (i + 1) * 128)
        both = jnp.concatenate([high_ref[rows, :], low_ref[rows, :]])
        by_high = dot16(both, high_ref[i * 128 :, :], NT)
        by_low = dot16(both, low_ref[i * 128 :, :], NT)
        product = (by_high[128:] + by_low[:128] + by_low[128:]) + by_high[:128]
        for j in range(i, 5):
            block = product[:, (j - i) * 128 : (j - i + 1) * 128]
            if i == j:
                put(UPPER[i], block[:64])
                lower.append(block[64:])
            else:
                put(ACROSS[i, j], block[:64])
                put(ACROSS[i, j] + 1, block[64:])
    left = lax.broadcasted_iota(jnp.int32, (64, 128), 1) < 64
    put(25, jnp.where(left, pltpu.roll(lower[1], 64, 1), lower[0]))
    put(26, jnp.where(left, pltpu.roll(lower[3], 64, 1), lower[2]))
    put(27, lower[4])
    for copy in copies:
        copy.wait()


def local_gram(core, held):
    flat = jax.ShapeDtypeStruct((640, held.shape[1] * 128), BF)
    return pl.pallas_call(
        gram_kernel,
        out_shape=(jax.ShapeDtypeStruct((2, 896, 128), F32), pltpu.HBM(flat.shape, BF), pltpu.HBM(flat.shape, BF)),
        in_specs=[SMEM, VMEM],
        out_specs=(VMEM, HBM, HBM),
        scratch_shapes=[
            pltpu.VMEM(flat.shape, BF),
            pltpu.VMEM(flat.shape, BF),
            pltpu.SemaphoreType.DMA((2,)),
        ],
        compiler_params=BIG,
    )(core, held)


def eliminate(panel, w_ref):
    count = NB // 8
    sides = range(len(panel))
    tiles = [[side[8 * t : 8 * t + 8] for t in range(count)] for side in panel]
    for j in range(0, NB, STEP):
        t0 = j // 8
        cols = [
            [
                jnp.broadcast_to(tiles[0][t][:, j + k : j + k + 1], (8, 128))
                for t in range(t0, count)
            ]
            for k in range(STEP)
        ]
        rows = [
            [tiles[s][(j + k) // 8][(j + k) % 8 : (j + k) % 8 + 1, :] for k in range(STEP)]
            for s in sides
        ]
        a = {
            (i, k): cols[k][(j + i) // 8 - t0][(j + i) % 8 : (j + i) % 8 + 1, :]
            for k in range(STEP)
            for i in range(k, STEP)
        }
        for k in range(STEP):
            scale = lax.rsqrt(a[k, k])
            for i in range(k + 1, STEP):
                a[i, k] = a[i, k] * scale
            for i in range(k + 1, STEP):
                for m in range(k + 1, i + 1):
                    a[i, m] = a[i, m] - a[i, k] * a[m, k]
            for s in sides:
                rows[s][k] = rows[s][k] * scale
                for i in range(k + 1, STEP):
                    rows[s][i] = rows[s][i] - a[i, k] * rows[s][k]
                w_ref[j + k : j + k + 1, 128 * s : 128 * s + 128] = rows[s][k]
            cols[k] = [c * scale for c in cols[k]]
            for i in range(k + 1, STEP):
                cols[i] = [c - a[i, k] * w for c, w in zip(cols[i], cols[k])]
        for t in range((j + STEP) // 8, count):
            for s in sides:
                change = cols[0][t - t0] * rows[s][0]
                for k in range(1, STEP):
                    change = change + cols[k][t - t0] * rows[s][k]
                tiles[s][t] = tiles[s][t] - change


def orthonormalize(a_ref, t_ref, w_ref):
    rank = t_ref.shape[0]
    lane = lax.broadcasted_iota(jnp.int32, (NB, 128), 1)
    row = lax.broadcasted_iota(jnp.int32, (NB, 128), 0)
    for k in range(rank // NB):
        own = slice(k * NB, (k + 1) * NB)
        rest = (k + 1) * NB
        n = rank - k * NB
        w = w_ref.at[k % 2]
        left = a_ref[own, :128]
        if n + NB <= 128:
            at = n
            panel = [jnp.where(lane < n, left, jnp.where(lane - n == row, 1.0, 0.0))]
        else:
            at = max(n, 128)
            right = jnp.where(lane - (at - 128) == row, 1.0, 0.0)
            if n > 128:
                right = jnp.where(lane < n - 128, a_ref[own, 128:], right)
            panel = [left, right]
        eliminate(panel, w)
        inverse = w[:, at : at + NB]
        if rest < rank:
            after = pltpu.roll(w[...], 256 - NB, 1)[:, :128]
            moved = pltpu.roll(a_ref[rest:, :], 256 - NB, 1)[:, :128]
            a_ref[rest:, :128] = moved - dot(after[:, : n - NB], after, TN)
        solved = dot(inverse, t_ref[own, :])
        t_ref[own, :] = solved
        if rest < rank:
            t_ref[rest:, :] = t_ref[rest:, :] - dot(after[:, : n - NB], solved, TN)


def subspace_kernel(
    packed_ref,
    start_ref,
    high_in,
    low_in,
    basis_out,
    core_out,
    g_ref,
    a_ref,
    t_ref,
    w_ref,
    high_ref,
    low_ref,
    core_ref,
    sem,
):
    rank = start_ref.shape[0]
    pairs = high_ref.shape[1] // 256
    loads = [
        pltpu.make_async_copy(high_in, high_ref, sem.at[0]),
        pltpu.make_async_copy(low_in, low_ref, sem.at[1]),
    ]
    for copy in loads:
        copy.start()
    for (i, j), at in ACROSS.items():
        block = packed_ref[at * 64 : at * 64 + 128, :]
        g_ref[i * 128 : (i + 1) * 128, j * 128 : (j + 1) * 128] = block
        g_ref[j * 128 : (j + 1) * 128, i * 128 : (i + 1) * 128] = block.T
    right = lax.broadcasted_iota(jnp.int32, (64, 128), 1) >= 64
    for i in range(5):
        upper = packed_ref[UPPER[i] * 64 : UPPER[i] * 64 + 64, :]
        lower = packed_ref[(25 + i // 2) * 64 : (26 + i // 2) * 64, :]
        if i % 2:
            lower = pltpu.roll(lower, 64, 1)
        turned = jnp.concatenate([upper, upper]).T[64:]
        square = slice(i * 128, (i + 1) * 128)
        g_ref[square, square] = jnp.concatenate([upper, jnp.where(right, lower, turned)])
    t_ref[...] = start_ref[...]
    a_ref[...] = jnp.zeros_like(a_ref)
    for _ in range(ITERS):
        image = dot(t_ref[...], g_ref[...])
        t_ref[...] = image
        a_ref[:, :rank] = dot(image, image, NT)
        orthonormalize(a_ref, t_ref, w_ref)
    basis = t_ref[...]
    stores = [pltpu.make_async_copy(t_ref, basis_out, sem.at[2])]
    stores[0].start()
    for copy in loads:
        copy.wait()
    high, low = halves(basis)
    both = jnp.concatenate([high, low])
    for q in range(pairs):
        lanes = slice(q * 256, (q + 1) * 256)
        by_high = dot16(both, high_ref[:, lanes])
        by_low = dot16(high, low_ref[:, lanes])
        product = (by_high[rank:] + by_low) + by_high[:rank]
        core_ref[2 * q] = product[:, :128]
        core_ref[2 * q + 1] = product[:, 128:]
        two = pl.ds(2 * q, 2)
        stores.append(pltpu.make_async_copy(core_ref.at[two], core_out.at[two], sem.at[3 + q]))
        stores[-1].start()
    for copy in stores:
        copy.wait()


def subspace_and_core(packed, start, high, low):
    rank, rows = start.shape
    cells = high.shape[1] // 128
    return pl.pallas_call(
        subspace_kernel,
        out_shape=(
            jax.ShapeDtypeStruct((rank, rows), F32),
            jax.ShapeDtypeStruct((cells, rank, 128), F32),
        ),
        in_specs=[VMEM, VMEM, HBM, HBM],
        out_specs=(HBM, HBM),
        scratch_shapes=[
            pltpu.VMEM((rows, rows), F32),
            pltpu.VMEM((rank, 256), F32),
            pltpu.VMEM((rank, rows), F32),
            pltpu.VMEM((2, NB, 256), F32),
            pltpu.VMEM(high.shape, BF),
            pltpu.VMEM(low.shape, BF),
            pltpu.VMEM((cells, rank, 128), F32),
            pltpu.SemaphoreType.DMA((3 + cells // 2,)),
        ],
        compiler_params=BIG,
    )(packed, start, *(pltpu.with_memory_space_constraint(v, pltpu.HBM) for v in (high, low)))


def exchange(pieces, axes):
    return lax.all_to_all(pieces, axes, 0, 0, tiled=True)


def shards(field, start):
    with jax.named_scope("regroup"):
        core = lax.axis_index("c").astype(jnp.int32).reshape(1)
        pieces = regroup(field).reshape(16, 10, 40, 128)
        pieces, core = lax.optimization_barrier((pieces, core))
        held = exchange(pieces, FIBRE)
    with jax.named_scope("gram"):
        parts, high, low = local_gram(core, held)
    with jax.named_scope("reduce_pair"):
        mine = parts[0] + lax.ppermute(parts[1], "c", SWAP)
    with jax.named_scope("reduce_plane"):
        mine = exchange(mine.reshape(32, 7, 4, 128), PLANE).sum(0)
    with jax.named_scope("sum_line"):
        mine = exchange(jnp.broadcast_to(mine, (8, 7, 4, 128)), "y").sum(0)
    with jax.named_scope("gather_plane"):
        mine = exchange(jnp.broadcast_to(mine, (32, 7, 4, 128)), PLANE)
    with jax.named_scope("gather_pair"):
        packed = lax.all_gather(mine.reshape(896, 128), "c", axis=0, tiled=True)
    with jax.named_scope("subspace"):
        basis, core = subspace_and_core(packed, start.T, high, low)
    return basis.T, core.transpose(1, 0, 2)


def solution(mesh):
    inner = jax.sharding.Mesh(mesh.devices.reshape(8, 2, 4, 8), ("y", "c", "x", "z"))
    return jax.shard_map(
        shards,
        mesh=inner,
        in_specs=(P(FIBRE, None, ("x", "z")), P()),
        out_specs=(P(), P(None, FIBRE, ("x", "z"))),
        check_vma=False,
    )
```

```python
import functools

import jax
import jax.numpy as jnp
from jax import lax
from jax.experimental import pallas as pl
from jax.experimental.pallas import tpu as pltpu
from jax.sharding import PartitionSpec as P

ITERS = 2
FIBRE = ("y", "c")
PLANE = ("x", "z")
SWAP = [(0, 1), (1, 0)]
NB = 80
STEP = 8
UPPER = [20, 21, 22, 23, 24]
ACROSS = {
    pair: 2 * at
    for at, pair in enumerate((i, j) for i in range(5) for j in range(i + 1, 5))
}
VMEM = pl.BlockSpec(memory_space=pltpu.VMEM)
HBM = pl.BlockSpec(memory_space=pltpu.HBM)
SMEM = pl.BlockSpec(memory_space=pltpu.SMEM)
BIG = pltpu.CompilerParams(vmem_limit_bytes=24 << 20)
BF = jnp.bfloat16
F32 = jnp.float32
NN = (((1,), (0,)), ((), ()))
NT = (((1,), (1,)), ((), ()))
TN = (((0,), (0,)), ((), ()))


def dot(a, b, dims=NN):
    return lax.dot_general(
        a, b, dims, precision=lax.Precision.HIGHEST, preferred_element_type=F32
    )


def dot16(a, b, dims=NN):
    return lax.dot_general(a, b, dims, preferred_element_type=F32)


def halves(x):
    high = x.astype(BF)
    return high, (x - high.astype(F32)).astype(BF)


def regroup_kernel(field_ref, out_ref, in_ref, sem):
    parts = field_ref.shape[0] // 8
    copies = []
    for part in range(parts):
        rows = pl.ds(8 * part, 8)
        copies.append(
            pltpu.make_async_copy(field_ref.at[rows], in_ref.at[rows], sem.at[part])
        )
        copies[-1].start()
    for part, copy in enumerate(copies):
        copy.wait()
        rows = slice(8 * part, 8 * part + 8)
        out_ref[:, rows, :] = jnp.swapaxes(in_ref[rows], 0, 1)


def regroup(field):
    rows, cells, lanes = field.shape
    return pl.pallas_call(
        regroup_kernel,
        out_shape=jax.ShapeDtypeStruct((cells, rows, lanes), F32),
        in_specs=[HBM],
        out_specs=VMEM,
        scratch_shapes=[pltpu.VMEM(field.shape, F32), pltpu.SemaphoreType.DMA((rows // 8,))],
        compiler_params=BIG,
    )(pltpu.with_memory_space_constraint(field, pltpu.HBM))


def gram_kernel(core_ref, held_ref, out_ref, high_out, low_out, high_ref, low_ref, sem):
    cells = held_ref.shape[1]
    copies = []
    for group in range(2):
        first, last = group * cells // 2, (group + 1) * cells // 2
        for p in range(first, last):
            x = held_ref[:, p].reshape(640, 128)
            lanes = slice(p * 128, (p + 1) * 128)
            high_ref[:, lanes], low_ref[:, lanes] = halves(x)
        lanes = pl.ds(first * 128, (last - first) * 128)
        for at, (source, target) in enumerate(((high_ref, high_out), (low_ref, low_out))):
            copies.append(
                pltpu.make_async_copy(
                    source.at[:, lanes], target.at[:, lanes], sem.at[2 * group + at]
                )
            )
            copies[-1].start()
    core = core_ref[0]

    def put(strip, value):
        at = strip % 14 * 64
        out_ref[core if strip < 14 else 1 - core, at : at + 64, :] = value

    lower = []
    for i in range(5):
        rows = slice(i * 128, (i + 1) * 128)
        both = jnp.concatenate([high_ref[rows, :], low_ref[rows, :]])
        by_high = dot16(both, high_ref[i * 128 :, :], NT)
        by_low = dot16(both, low_ref[i * 128 :, :], NT)
        product = (by_high[128:] + by_low[:128] + by_low[128:]) + by_high[:128]
        for j in range(i, 5):
            block = product[:, (j - i) * 128 : (j - i + 1) * 128]
            if i == j:
                put(UPPER[i], block[:64])
                lower.append(block[64:])
            else:
                put(ACROSS[i, j], block[:64])
                put(ACROSS[i, j] + 1, block[64:])
    left = lax.broadcasted_iota(jnp.int32, (64, 128), 1) < 64
    put(25, jnp.where(left, pltpu.roll(lower[1], 64, 1), lower[0]))
    put(26, jnp.where(left, pltpu.roll(lower[3], 64, 1), lower[2]))
    put(27, lower[4])
    for copy in copies:
        copy.wait()


def local_gram(core, held):
    flat = jax.ShapeDtypeStruct((640, held.shape[1] * 128), BF)
    return pl.pallas_call(
        gram_kernel,
        out_shape=(jax.ShapeDtypeStruct((2, 896, 128), F32), pltpu.HBM(flat.shape, BF), pltpu.HBM(flat.shape, BF)),
        in_specs=[SMEM, VMEM],
        out_specs=(VMEM, HBM, HBM),
        scratch_shapes=[
            pltpu.VMEM(flat.shape, BF),
            pltpu.VMEM(flat.shape, BF),
            pltpu.SemaphoreType.DMA((4,)),
        ],
        compiler_params=BIG,
    )(core, held)


def eliminate(panel, w_ref):
    count = NB // 8
    sides = range(len(panel))
    tiles = [[side[8 * t : 8 * t + 8] for t in range(count)] for side in panel]
    for j in range(0, NB, STEP):
        t0 = j // 8
        cols = [
            [
                jnp.broadcast_to(tiles[0][t][:, j + k : j + k + 1], (8, 128))
                for t in range(t0, count)
            ]
            for k in range(STEP)
        ]
        rows = [
            [tiles[s][(j + k) // 8][(j + k) % 8 : (j + k) % 8 + 1, :] for k in range(STEP)]
            for s in sides
        ]
        a = {
            (i, k): cols[k][(j + i) // 8 - t0][(j + i) % 8 : (j + i) % 8 + 1, :]
            for k in range(STEP)
            for i in range(k, STEP)
        }
        for k in range(STEP):
            scale = lax.rsqrt(a[k, k])
            for i in range(k + 1, STEP):
                a[i, k] = a[i, k] * scale
            for i in range(k + 1, STEP):
                for m in range(k + 1, i + 1):
                    a[i, m] = a[i, m] - a[i, k] * a[m, k]
            for s in sides:
                rows[s][k] = rows[s][k] * scale
                for i in range(k + 1, STEP):
                    rows[s][i] = rows[s][i] - a[i, k] * rows[s][k]
                w_ref[j + k : j + k + 1, 128 * s : 128 * s + 128] = rows[s][k]
            cols[k] = [c * scale for c in cols[k]]
            for i in range(k + 1, STEP):
                cols[i] = [c - a[i, k] * w for c, w in zip(cols[i], cols[k])]
        for t in range((j + STEP) // 8, count):
            for s in sides:
                change = cols[0][t - t0] * rows[s][0]
                for k in range(1, STEP):
                    change = change + cols[k][t - t0] * rows[s][k]
                tiles[s][t] = tiles[s][t] - change


def orthonormalize(a_ref, t_ref, w_ref):
    rank = t_ref.shape[0]
    lane = lax.broadcasted_iota(jnp.int32, (NB, 128), 1)
    row = lax.broadcasted_iota(jnp.int32, (NB, 128), 0)
    for k in range(rank // NB):
        own = slice(k * NB, (k + 1) * NB)
        rest = (k + 1) * NB
        n = rank - k * NB
        w = w_ref.at[k % 2]
        left = a_ref[own, :128]
        if n + NB <= 128:
            at = n
            panel = [jnp.where(lane < n, left, jnp.where(lane - n == row, 1.0, 0.0))]
        else:
            at = max(n, 128)
            right = jnp.where(lane - (at - 128) == row, 1.0, 0.0)
            if n > 128:
                right = jnp.where(lane < n - 128, a_ref[own, 128:], right)
            panel = [left, right]
        eliminate(panel, w)
        inverse = w[:, at : at + NB]
        if rest < rank:
            after = pltpu.roll(w[...], 256 - NB, 1)[:, :128]
            moved = pltpu.roll(a_ref[rest:, :], 256 - NB, 1)[:, :128]
            a_ref[rest:, :128] = moved - dot(after[:, : n - NB], after, TN)
        solved = dot(inverse, t_ref[own, :])
        t_ref[own, :] = solved
        if rest < rank:
            t_ref[rest:, :] = t_ref[rest:, :] - dot(after[:, : n - NB], solved, TN)


def subspace_kernel(
    packed_ref,
    start_ref,
    high_in,
    low_in,
    basis_out,
    core_out,
    g_ref,
    a_ref,
    t_ref,
    w_ref,
    high_ref,
    low_ref,
    core_ref,
    sem,
):
    rank = start_ref.shape[0]
    pairs = high_ref.shape[1] // 256
    loads = [
        pltpu.make_async_copy(high_in, high_ref, sem.at[0]),
        pltpu.make_async_copy(low_in, low_ref, sem.at[1]),
    ]
    for copy in loads:
        copy.start()
    for (i, j), at in ACROSS.items():
        block = packed_ref[at * 64 : at * 64 + 128, :]
        g_ref[i * 128 : (i + 1) * 128, j * 128 : (j + 1) * 128] = block
        g_ref[j * 128 : (j + 1) * 128, i * 128 : (i + 1) * 128] = block.T
    right = lax.broadcasted_iota(jnp.int32, (64, 128), 1) >= 64
    for i in range(5):
        upper = packed_ref[UPPER[i] * 64 : UPPER[i] * 64 + 64, :]
        lower = packed_ref[(25 + i // 2) * 64 : (26 + i // 2) * 64, :]
        if i % 2:
            lower = pltpu.roll(lower, 64, 1)
        turned = jnp.concatenate([upper, upper]).T[64:]
        square = slice(i * 128, (i + 1) * 128)
        g_ref[square, square] = jnp.concatenate([upper, jnp.where(right, lower, turned)])
    t_ref[...] = start_ref[...]
    a_ref[...] = jnp.zeros_like(a_ref)
    for _ in range(ITERS):
        image = dot(t_ref[...], g_ref[...])
        t_ref[...] = image
        a_ref[:, :rank] = dot(image, image, NT)
        orthonormalize(a_ref, t_ref, w_ref)
    basis = t_ref[...]
    stores = [pltpu.make_async_copy(t_ref, basis_out, sem.at[2])]
    stores[0].start()
    for copy in loads:
        copy.wait()
    high, low = halves(basis)
    both = jnp.concatenate([high, low])
    for q in range(pairs):
        lanes = slice(q * 256, (q + 1) * 256)
        by_high = dot16(both, high_ref[:, lanes])
        by_low = dot16(high, low_ref[:, lanes])
        product = (by_high[rank:] + by_low) + by_high[:rank]
        core_ref[2 * q] = product[:, :128]
        core_ref[2 * q + 1] = product[:, 128:]
        two = pl.ds(2 * q, 2)
        stores.append(pltpu.make_async_copy(core_ref.at[two], core_out.at[two], sem.at[3 + q]))
        stores[-1].start()
    for copy in stores:
        copy.wait()


def subspace_and_core(packed, start, high, low):
    rank, rows = start.shape
    cells = high.shape[1] // 128
    return pl.pallas_call(
        subspace_kernel,
        out_shape=(
            jax.ShapeDtypeStruct((rank, rows), F32),
            jax.ShapeDtypeStruct((cells, rank, 128), F32),
        ),
        in_specs=[VMEM, VMEM, HBM, HBM],
        out_specs=(HBM, HBM),
        scratch_shapes=[
            pltpu.VMEM((rows, rows), F32),
            pltpu.VMEM((rank, 256), F32),
            pltpu.VMEM((rank, rows), F32),
            pltpu.VMEM((2, NB, 256), F32),
            pltpu.VMEM(high.shape, BF),
            pltpu.VMEM(low.shape, BF),
            pltpu.VMEM((cells, rank, 128), F32),
            pltpu.SemaphoreType.DMA((3 + cells // 2,)),
        ],
        compiler_params=BIG,
    )(packed, start, *(pltpu.with_memory_space_constraint(v, pltpu.HBM) for v in (high, low)))


def exchange(pieces, axes):
    return lax.all_to_all(pieces, axes, 0, 0, tiled=True)


def shards(field, start):
    with jax.named_scope("regroup"):
        core = lax.axis_index("c").astype(jnp.int32).reshape(1)
        pieces = regroup(field).reshape(16, 10, 40, 128)
        pieces, core = lax.optimization_barrier((pieces, core))
        held = exchange(pieces, FIBRE)
    with jax.named_scope("gram"):
        parts, high, low = local_gram(core, held)
    with jax.named_scope("reduce_pair"):
        mine = parts[0] + lax.ppermute(parts[1], "c", SWAP)
    with jax.named_scope("reduce_plane"):
        mine = exchange(mine.reshape(32, 7, 4, 128), PLANE).sum(0)
    with jax.named_scope("sum_line"):
        mine = exchange(jnp.broadcast_to(mine, (8, 7, 4, 128)), "y").sum(0)
    with jax.named_scope("gather_plane"):
        mine = exchange(jnp.broadcast_to(mine, (32, 7, 4, 128)), PLANE)
    with jax.named_scope("gather_pair"):
        packed = lax.all_gather(mine.reshape(896, 128), "c", axis=0, tiled=True)
    with jax.named_scope("subspace"):
        basis, core = subspace_and_core(packed, start.T, high, low)
    return basis.T, core.transpose(1, 0, 2)


def solution(mesh):
    inner = jax.sharding.Mesh(mesh.devices.reshape(8, 2, 4, 8), ("y", "c", "x", "z"))
    return jax.shard_map(
        shards,
        mesh=inner,
        in_specs=(P(FIBRE, None, ("x", "z")), P()),
        out_specs=(P(), P(None, FIBRE, ("x", "z"))),
        check_vma=False,
    )
```

```python
import functools

import jax
import jax.numpy as jnp
from jax import lax
from jax.experimental import pallas as pl
from jax.experimental.pallas import tpu as pltpu
from jax.sharding import PartitionSpec as P

ITERS = 2
FIBRE = ("y", "c")
SENT = ("c", "y")
PLACE = [f % 2 * 8 + f // 2 for f in range(16)]
PLANE = ("z", "x")
SWAP = [(0, 1), (1, 0)]
NB = 80
STEP = 8
UPPER = [20, 21, 22, 23, 24]
ACROSS = {
    pair: 2 * at
    for at, pair in enumerate((i, j) for i in range(5) for j in range(i + 1, 5))
}
VMEM = pl.BlockSpec(memory_space=pltpu.VMEM)
HBM = pl.BlockSpec(memory_space=pltpu.HBM)
SMEM = pl.BlockSpec(memory_space=pltpu.SMEM)
BIG = pltpu.CompilerParams(vmem_limit_bytes=24 << 20)
BF = jnp.bfloat16
F32 = jnp.float32
NN = (((1,), (0,)), ((), ()))
NT = (((1,), (1,)), ((), ()))
TN = (((0,), (0,)), ((), ()))


def dot(a, b, dims=NN):
    return lax.dot_general(
        a, b, dims, precision=lax.Precision.HIGHEST, preferred_element_type=F32
    )


def dot16(a, b, dims=NN):
    return lax.dot_general(a, b, dims, preferred_element_type=F32)


def halves(x):
    high = x.astype(BF)
    return high, (x - high.astype(F32)).astype(BF)


def regroup_kernel(field_ref, out_ref, in_ref, sem):
    parts = field_ref.shape[0] // 8
    copies = []
    for part in range(parts):
        rows = pl.ds(8 * part, 8)
        copies.append(
            pltpu.make_async_copy(field_ref.at[rows], in_ref.at[rows], sem.at[part])
        )
        copies[-1].start()
    for part, copy in enumerate(copies):
        copy.wait()
        rows = slice(8 * part, 8 * part + 8)
        turned = jnp.swapaxes(in_ref[rows], 0, 1)
        each = turned.shape[0] // 16
        for f, place in enumerate(PLACE):
            out_ref[place * each : (place + 1) * each, rows, :] = turned[
                f * each : (f + 1) * each
            ]


def regroup(field):
    rows, cells, lanes = field.shape
    return pl.pallas_call(
        regroup_kernel,
        out_shape=jax.ShapeDtypeStruct((cells, rows, lanes), F32),
        in_specs=[HBM],
        out_specs=VMEM,
        scratch_shapes=[pltpu.VMEM(field.shape, F32), pltpu.SemaphoreType.DMA((rows // 8,))],
        compiler_params=BIG,
    )(pltpu.with_memory_space_constraint(field, pltpu.HBM))


def gram_kernel(core_ref, held_ref, out_ref, high_out, low_out, high_ref, low_ref, sem):
    cells = held_ref.shape[1]
    copies = []
    for group in range(2):
        first, last = group * cells // 2, (group + 1) * cells // 2
        for p in range(first, last):
            x = jnp.concatenate([held_ref[place, p] for place in PLACE])
            lanes = slice(p * 128, (p + 1) * 128)
            high_ref[:, lanes], low_ref[:, lanes] = halves(x)
        lanes = pl.ds(first * 128, (last - first) * 128)
        for at, (source, target) in enumerate(((high_ref, high_out), (low_ref, low_out))):
            copies.append(
                pltpu.make_async_copy(
                    source.at[:, lanes], target.at[:, lanes], sem.at[2 * group + at]
                )
            )
            copies[-1].start()
    core = core_ref[0]

    def put(strip, value):
        at = strip % 14 * 64
        out_ref[core if strip < 14 else 1 - core, at : at + 64, :] = value

    lower = []
    for i in range(5):
        rows = slice(i * 128, (i + 1) * 128)
        both = jnp.concatenate([high_ref[rows, :], low_ref[rows, :]])
        by_high = dot16(both, high_ref[i * 128 :, :], NT)
        by_low = dot16(both, low_ref[i * 128 :, :], NT)
        product = (by_high[128:] + by_low[:128] + by_low[128:]) + by_high[:128]
        for j in range(i, 5):
            block = product[:, (j - i) * 128 : (j - i + 1) * 128]
            if i == j:
                put(UPPER[i], block[:64])
                lower.append(block[64:])
            else:
                put(ACROSS[i, j], block[:64])
                put(ACROSS[i, j] + 1, block[64:])
    left = lax.broadcasted_iota(jnp.int32, (64, 128), 1) < 64
    put(25, jnp.where(left, pltpu.roll(lower[1], 64, 1), lower[0]))
    put(26, jnp.where(left, pltpu.roll(lower[3], 64, 1), lower[2]))
    put(27, lower[4])
    for copy in copies:
        copy.wait()


def local_gram(core, held):
    flat = jax.ShapeDtypeStruct((640, held.shape[1] * 128), BF)
    return pl.pallas_call(
        gram_kernel,
        out_shape=(jax.ShapeDtypeStruct((2, 896, 128), F32), pltpu.HBM(flat.shape, BF), pltpu.HBM(flat.shape, BF)),
        in_specs=[SMEM, VMEM],
        out_specs=(VMEM, HBM, HBM),
        scratch_shapes=[
            pltpu.VMEM(flat.shape, BF),
            pltpu.VMEM(flat.shape, BF),
            pltpu.SemaphoreType.DMA((4,)),
        ],
        compiler_params=BIG,
    )(core, held)


def eliminate(panel, w_ref):
    count = NB // 8
    sides = range(len(panel))
    tiles = [[side[8 * t : 8 * t + 8] for t in range(count)] for side in panel]
    for j in range(0, NB, STEP):
        t0 = j // 8
        cols = [
            [
                jnp.broadcast_to(tiles[0][t][:, j + k : j + k + 1], (8, 128))
                for t in range(t0, count)
            ]
            for k in range(STEP)
        ]
        rows = [
            [tiles[s][(j + k) // 8][(j + k) % 8 : (j + k) % 8 + 1, :] for k in range(STEP)]
            for s in sides
        ]
        a = {
            (i, k): cols[k][(j + i) // 8 - t0][(j + i) % 8 : (j + i) % 8 + 1, :]
            for k in range(STEP)
            for i in range(k, STEP)
        }
        for k in range(STEP):
            scale = lax.rsqrt(a[k, k])
            for i in range(k + 1, STEP):
                a[i, k] = a[i, k] * scale
            for i in range(k + 1, STEP):
                for m in range(k + 1, i + 1):
                    a[i, m] = a[i, m] - a[i, k] * a[m, k]
            for s in sides:
                rows[s][k] = rows[s][k] * scale
                for i in range(k + 1, STEP):
                    rows[s][i] = rows[s][i] - a[i, k] * rows[s][k]
                w_ref[j + k : j + k + 1, 128 * s : 128 * s + 128] = rows[s][k]
            cols[k] = [c * scale for c in cols[k]]
            for i in range(k + 1, STEP):
                cols[i] = [c - a[i, k] * w for c, w in zip(cols[i], cols[k])]
        for t in range((j + STEP) // 8, count):
            for s in sides:
                change = cols[0][t - t0] * rows[s][0]
                for k in range(1, STEP):
                    change = change + cols[k][t - t0] * rows[s][k]
                tiles[s][t] = tiles[s][t] - change


def orthonormalize(a_ref, t_ref, w_ref):
    rank = t_ref.shape[0]
    lane = lax.broadcasted_iota(jnp.int32, (NB, 128), 1)
    row = lax.broadcasted_iota(jnp.int32, (NB, 128), 0)
    for k in range(rank // NB):
        own = slice(k * NB, (k + 1) * NB)
        rest = (k + 1) * NB
        n = rank - k * NB
        w = w_ref.at[k % 2]
        left = a_ref[own, :128]
        if n + NB <= 128:
            at = n
            panel = [jnp.where(lane < n, left, jnp.where(lane - n == row, 1.0, 0.0))]
        else:
            at = max(n, 128)
            right = jnp.where(lane - (at - 128) == row, 1.0, 0.0)
            if n > 128:
                right = jnp.where(lane < n - 128, a_ref[own, 128:], right)
            panel = [left, right]
        eliminate(panel, w)
        inverse = w[:, at : at + NB]
        if rest < rank:
            after = pltpu.roll(w[...], 256 - NB, 1)[:, :128]
            moved = pltpu.roll(a_ref[rest:, :], 256 - NB, 1)[:, :128]
            a_ref[rest:, :128] = moved - dot(after[:, : n - NB], after, TN)
        solved = dot(inverse, t_ref[own, :])
        t_ref[own, :] = solved
        if rest < rank:
            t_ref[rest:, :] = t_ref[rest:, :] - dot(after[:, : n - NB], solved, TN)


def subspace_kernel(
    packed_ref,
    start_ref,
    high_in,
    low_in,
    basis_out,
    core_out,
    g_ref,
    a_ref,
    t_ref,
    w_ref,
    high_ref,
    low_ref,
    core_ref,
    sem,
):
    rank = start_ref.shape[0]
    pairs = high_ref.shape[1] // 256
    loads = [
        pltpu.make_async_copy(high_in, high_ref, sem.at[0]),
        pltpu.make_async_copy(low_in, low_ref, sem.at[1]),
    ]
    for copy in loads:
        copy.start()
    for (i, j), at in ACROSS.items():
        block = packed_ref[at * 64 : at * 64 + 128, :]
        g_ref[i * 128 : (i + 1) * 128, j * 128 : (j + 1) * 128] = block
        g_ref[j * 128 : (j + 1) * 128, i * 128 : (i + 1) * 128] = block.T
    right = lax.broadcasted_iota(jnp.int32, (64, 128), 1) >= 64
    for i in range(5):
        upper = packed_ref[UPPER[i] * 64 : UPPER[i] * 64 + 64, :]
        lower = packed_ref[(25 + i // 2) * 64 : (26 + i // 2) * 64, :]
        if i % 2:
            lower = pltpu.roll(lower, 64, 1)
        turned = jnp.concatenate([upper, upper]).T[64:]
        square = slice(i * 128, (i + 1) * 128)
        g_ref[square, square] = jnp.concatenate([upper, jnp.where(right, lower, turned)])
    t_ref[...] = start_ref[...]
    a_ref[...] = jnp.zeros_like(a_ref)
    for _ in range(ITERS):
        image = dot(t_ref[...], g_ref[...])
        t_ref[...] = image
        a_ref[:, :rank] = dot(image, image, NT)
        orthonormalize(a_ref, t_ref, w_ref)
    basis = t_ref[...]
    stores = [pltpu.make_async_copy(t_ref, basis_out, sem.at[2])]
    stores[0].start()
    for copy in loads:
        copy.wait()
    high, low = halves(basis)
    both = jnp.concatenate([high, low])
    for q in range(pairs):
        lanes = slice(q * 256, (q + 1) * 256)
        by_high = dot16(both, high_ref[:, lanes])
        by_low = dot16(high, low_ref[:, lanes])
        product = (by_high[rank:] + by_low) + by_high[:rank]
        core_ref[2 * q] = product[:, :128]
        core_ref[2 * q + 1] = product[:, 128:]
        two = pl.ds(2 * q, 2)
        stores.append(pltpu.make_async_copy(core_ref.at[two], core_out.at[two], sem.at[3 + q]))
        stores[-1].start()
    for copy in stores:
        copy.wait()


def subspace_and_core(packed, start, high, low):
    rank, rows = start.shape
    cells = high.shape[1] // 128
    return pl.pallas_call(
        subspace_kernel,
        out_shape=(
            jax.ShapeDtypeStruct((rank, rows), F32),
            jax.ShapeDtypeStruct((cells, rank, 128), F32),
        ),
        in_specs=[VMEM, VMEM, HBM, HBM],
        out_specs=(HBM, HBM),
        scratch_shapes=[
            pltpu.VMEM((rows, rows), F32),
            pltpu.VMEM((rank, 256), F32),
            pltpu.VMEM((rank, rows), F32),
            pltpu.VMEM((2, NB, 256), F32),
            pltpu.VMEM(high.shape, BF),
            pltpu.VMEM(low.shape, BF),
            pltpu.VMEM((cells, rank, 128), F32),
            pltpu.SemaphoreType.DMA((3 + cells // 2,)),
        ],
        compiler_params=BIG,
    )(packed, start, *(pltpu.with_memory_space_constraint(v, pltpu.HBM) for v in (high, low)))


def exchange(pieces, axes):
    return lax.all_to_all(pieces, axes, 0, 0, tiled=True)


def shards(field, start):
    with jax.named_scope("regroup"):
        core = lax.axis_index("c").astype(jnp.int32).reshape(1)
        pieces = regroup(field).reshape(16, 10, 40, 128)
        pieces, core = lax.optimization_barrier((pieces, core))
        held = exchange(pieces, SENT)
    with jax.named_scope("gram"):
        parts, high, low = local_gram(core, held)
    with jax.named_scope("reduce_pair"):
        mine = parts[0] + lax.ppermute(parts[1], "c", SWAP)
    with jax.named_scope("reduce_plane"):
        mine = exchange(mine.reshape(32, 7, 4, 128), PLANE).sum(0)
    with jax.named_scope("sum_line"):
        mine = exchange(jnp.broadcast_to(mine, (8, 7, 4, 128)), "y").sum(0)
    with jax.named_scope("gather_plane"):
        mine = exchange(jnp.broadcast_to(mine, (32, 7, 4, 128)), PLANE)
    with jax.named_scope("gather_pair"):
        packed = lax.all_gather(mine.reshape(896, 128), "c", axis=0, tiled=True)
    with jax.named_scope("subspace"):
        basis, core = subspace_and_core(packed, start.T, high, low)
    return basis.T, core.transpose(1, 0, 2)


def solution(mesh):
    inner = jax.sharding.Mesh(mesh.devices.reshape(8, 2, 4, 8), ("y", "c", "x", "z"))
    return jax.shard_map(
        shards,
        mesh=inner,
        in_specs=(P(FIBRE, None, ("x", "z")), P()),
        out_specs=(P(), P(None, FIBRE, ("x", "z"))),
        check_vma=False,
    )
```
